32 devices in a mesh: site: 2 (over y), pt: 4 (over z), var: 2 (over x), cmp: 2 (over core).
Axes of the slice: x: 2, y: 2, z: 4, core: 2. Of those that a mesh axis runs over, the one named last changes fastest.
Arguments:
- strain_green: bfloat16 [5120, 24, 256], P(('site', 'pt'), None, 'cmp'), parts along dimension 0, may hold values from -2.390625 to 2.390625
- green_scale: float32 [40, 24], P(('site', 'pt')), parts along dimension 0, may hold values from 0.3 to 3
- mechanism: float32 [6, 2560], P(None, 'pt'), may hold values from -4 to 4
- slip_amplitude: bfloat16 [4, 32, 1536], P('pt', 'var'), may hold values from 0.19921875 to 2
- onset_time: float32 [4, 32, 1536], P('pt', 'var'), may hold values from 0 to 128
- rupture_row: int32 [4], replicated, may hold values from 0 to 3, each once
- rupture_blocks: int32 [4, 12], replicated, may hold values from 0 to 19, as said below
- block_count: int32 [4], replicated, may hold values from 1 to 12, 16 in all
- crossover: int32 [4], replicated, may hold values from 128 to 251
- high_band: float32 [8, 32, 2, 512], P(('site', 'pt'), 'var', None, 'cmp'), parts along dimension 0, may hold values from -6 to 6
Outputs:
- seismograms: float32 [8, 32, 2, 512], P(('site', 'pt'), 'var', None, 'cmp'), parts along dimension 0
The draws below stay inside these ranges and needn't reach their ends.
There are 2 independent parts, one for each index of `site`. The reference program is written for one: setup_inputs(seed, part) draws one part's arguments, and reference() takes and returns one part's arrays. A program takes and returns all parts, laid end to end along the dimension named above; an argument that names none is the same for every part. Nothing has to cross between parts.
Inputs may be any that keep to these rules, and one draw needn't show every extreme that they name: `rupture_blocks`: each row names 12 different point blocks; rupture r covers the first block_count[r] of them.
All inputs are finite; a program needn't handle non-finite values.
Results may differ from the reference program's by a relative error of at most 0.0028.
Values may be sent and summed in bfloat16 or wider, within the bound.
A program may use at most 64 MiB of HBM per device.

```python
import math
import jax
import jax.numpy as jnp
import numpy as np
from jax import lax

BINS = 256
SAMPLES = 512
BLOCK = 128
MAXB = 12
NBLOCKS = 20
NPTS = 2560
RUPTURES = 4
VARS = 32


def draw_rupture_blocks(key, part):
    row_keys = jax.random.split(key, RUPTURES)
    shuffled = jax.vmap(lambda row_key: jax.random.permutation(row_key, NBLOCKS))(row_keys)
    return shuffled[:, :MAXB].astype(jnp.int32)


def plant(drawn, key, least, top_value):
    longest = drawn.shape.index(max(drawn.shape))
    spots = []
    for shift in (0, 1):
        where = [jax.random.randint(jax.random.fold_in(key, axis), (), 0, length) for axis, length in enumerate(drawn.shape)]
        where[longest] = (where[longest] + shift) % drawn.shape[longest]
        spots.append(tuple(where))
    return drawn.at[spots[0]].set(least).at[spots[1]].set(top_value)


def block_scale(rng, extent, shards, smallest, top_value):
    def one(dim, shards_of):
        draws = jax.random.uniform(jax.random.fold_in(jax.random.fold_in(rng, 6), dim), (shards_of,), jnp.float32, smallest / len(shards), top_value / len(shards))
        return jnp.repeat(jnp.exp(draws), extent[dim] // shards_of).reshape((-1,) + (1,) * (len(extent) - dim - 1))

    loudness = one(*shards[0])
    for cut in shards[1:]:
        loudness = loudness * one(*cut)
    return loudness


def profile(count, total, most, slope):
    portions = [(1 << 20) // math.isqrt(grade ** slope) + 1 for grade in range(2, count + 1)]
    rest, holding = total - most - (count - 1), [1] * (count - 1)
    while rest > 0:
        movable = [i for i in range(count - 1) if holding[i] < most]
        whole, remaining = sum([portions[i] for i in movable]), rest
        for i in movable:
            extra = min(most - holding[i], max(1, remaining * portions[i] // whole), rest)
            holding[i] = holding[i] + extra
            rest = rest - extra
    return np.array([most] + holding)


def uneven_parts(own_key, number_of, total, limit, lean):
    if number_of == 2:
        one = jax.random.randint(own_key, (), max(1, total - limit), min(limit, total - 1) + 1)
        return jnp.stack([one, total - one])
    sizes = jnp.asarray(profile(number_of, total, limit, lean), jnp.int32)
    couples = (number_of - 1) // 2
    source_of, receiver = sizes[1:1 + 2 * couples:2], sizes[2:2 + 2 * couples:2]
    slack = jnp.minimum(source_of - 1, limit - receiver)
    moved = jax.random.randint(jax.random.fold_in(own_key, 1), (couples,), 0, 1 << 20) % (slack + 1)
    sizes = sizes.at[1:1 + 2 * couples:2].set(source_of - moved).at[2:2 + 2 * couples:2].set(receiver + moved)
    return sizes[jax.random.permutation(jax.random.fold_in(own_key, 2), number_of)]


def centred(stream_key, extent, scale, limit, cuts=(), dtype=jnp.bfloat16):
    level = block_scale(stream_key, extent, cuts, -0.22, 0.18) if cuts else 1.0
    entries = jax.random.normal(stream_key, extent, jnp.float32) * scale * level
    return jnp.minimum(jnp.maximum(entries, -limit), limit).astype(dtype)


def setup_inputs(seed: int = 0, part: int = 0) -> dict:
    splits = jax.random.split(jax.random.key(seed), 11)
    part_splits = jax.random.split(jax.random.fold_in(splits[10], part), 11)
    return {
        "strain_green": centred(part_splits[0], (NPTS, 24, BINS), 0.3, 2.390625, ((0, 4), (2, 2))),
        "green_scale": jnp.clip(jnp.exp(math.log(3.0) - 2.3025851 * jax.random.uniform(part_splits[1], (NBLOCKS, 24), jnp.float32) ** block_scale(part_splits[1], (NBLOCKS, 24), ((0, 4),), -0.2, 0.2)), 0.3, 3.0),
        "mechanism": centred(splits[2], (6, NPTS), 1.0, 4.0, ((1, 4),), jnp.float32),
        "slip_amplitude": jnp.clip(jnp.exp(math.log(2.0) - 2.306499 * jax.random.uniform(splits[3], (RUPTURES, VARS, MAXB * BLOCK), jnp.float32) ** block_scale(splits[3], (RUPTURES, VARS, MAXB * BLOCK), ((0, 4), (1, 2)), -0.2, 0.2)), 0.19921875, 2.0).astype(jnp.bfloat16),
        "onset_time": jnp.clip(128.0 * jax.random.uniform(splits[4], (RUPTURES, VARS, MAXB * BLOCK), jnp.float32) ** block_scale(splits[4], (RUPTURES, VARS, MAXB * BLOCK), ((0, 4), (1, 2)), -0.2, 0.2), 0.0, 128.0),
        "rupture_row": jax.random.permutation(splits[5], RUPTURES).astype(jnp.int32),
        "rupture_blocks": draw_rupture_blocks(jax.random.fold_in(splits[10], 71), part),
        "block_count": uneven_parts(splits[7], RUPTURES, RUPTURES * (MAXB // 3), MAXB, 2).astype(jnp.int32),
        "crossover": plant(jax.random.randint(splits[8], (RUPTURES,), BINS // 2, BINS - 4), jax.random.fold_in(splits[8], 1), BINS // 2, (BINS - 4) - 1).astype(jnp.int32),
        "high_band": centred(part_splits[9], (RUPTURES, VARS, 2, SAMPLES), 1.0, 6.0, ((0, 4), (1, 2), (3, 2)), jnp.float32),
    }


taper_width = 8.0


def green_tensor(strain_green, green_scale, mechanism):
    points = strain_green.shape[0]
    bins_here = strain_green.shape[2]
    blocks_scale = jnp.repeat(green_scale, points // green_scale.shape[0], axis=0)
    factors = blocks_scale.reshape(points, 4, 6) * jnp.transpose(mechanism)[:, None, :]
    spectra = strain_green.reshape(points, 4, 6, bins_here).astype(jnp.float32)
    summed = jnp.einsum("pkjf,pkj->pkf", spectra, factors, precision=lax.Precision.HIGHEST)
    return summed.astype(jnp.bfloat16)


def block_term(green_block, amplitude, onset_block, phase_step):
    angles = onset_block[:, :, None] * phase_step[None, None, :]
    weight = amplitude.astype(jnp.float32)[:, :, None]
    with_cos = weight * jnp.cos(angles)
    with_sin = weight * jnp.sin(angles)
    green_wide = green_block.astype(jnp.float32)
    real_green = green_wide[:, 0:2]
    imag_green = green_wide[:, 2:4]
    highest = lax.Precision.HIGHEST
    real_part = jnp.einsum("vqf,qcf->vcf", with_cos, real_green, precision=highest) + jnp.einsum("vqf,qcf->vcf", with_sin, imag_green, precision=highest)
    imag_part = jnp.einsum("vqf,qcf->vcf", with_cos, imag_green, precision=highest) - jnp.einsum("vqf,qcf->vcf", with_sin, real_green, precision=highest)
    return jnp.concatenate([real_part, imag_part], axis=1)


def reference(strain_green, green_scale, mechanism, slip_amplitude, onset_time, rupture_row, rupture_blocks, block_count, crossover, high_band):
    highest = lax.Precision.HIGHEST
    green = green_tensor(strain_green, green_scale, mechanism)
    frequency = jnp.arange(BINS).astype(jnp.float32)
    phase_step = frequency * (2.0 * math.pi / SAMPLES)

    def one_row(position):
        rupture = rupture_row[position]
        blocks = rupture_blocks[rupture]
        covered = block_count[rupture]
        amplitudes = slip_amplitude[position]
        onsets = onset_time[position]

        def visit(running, slot_number):
            first_point = (blocks[slot_number] * BLOCK).astype(jnp.int32)
            green_block = lax.dynamic_slice_in_dim(green, first_point, BLOCK, 0)
            offset = (slot_number * BLOCK).astype(jnp.int32)
            amplitude = lax.dynamic_slice_in_dim(amplitudes, offset, BLOCK, 1)
            onset_block = lax.dynamic_slice_in_dim(onsets, offset, BLOCK, 1)
            contribution = block_term(green_block, amplitude, onset_block, phase_step)
            return running + jnp.where(slot_number < covered, contribution, jnp.zeros_like(contribution)), None

        running, unused = lax.scan(visit, jnp.zeros((VARS, 4, BINS), jnp.float32), jnp.arange(MAXB).astype(jnp.int32))
        return running

    spectrum = lax.map(one_row, jnp.arange(RUPTURES).astype(jnp.int32))
    samples_index = jnp.arange(SAMPLES).astype(jnp.int32)
    bins_index = jnp.arange(BINS).astype(jnp.int32)
    angles = ((bins_index[:, None] * samples_index[None, :]) % SAMPLES).astype(jnp.float32) * (2.0 * math.pi / SAMPLES)
    cosine = jnp.cos(angles)
    sine_table = jnp.sin(angles)
    band_rows = high_band.reshape(-1, SAMPLES)
    band_real = jnp.dot(band_rows, cosine.T, precision=highest)
    band_imag = -jnp.dot(band_rows, sine_table.T, precision=highest)
    crossing = crossover[rupture_row].astype(jnp.float32)
    taper_weight = jnp.clip((crossing[:, None] - frequency[None, :]) / taper_width + 0.5, 0.0, 1.0)
    taper_rows = jnp.repeat(taper_weight, VARS * 2, axis=0)
    spectrum_real = spectrum[:, :, 0:2].reshape(-1, BINS)
    spectrum_imag = spectrum[:, :, 2:4].reshape(-1, BINS)
    coefficient = jnp.where(bins_index == 0, 1.0, 2.0) / SAMPLES
    excess_real = taper_rows * (spectrum_real - band_real) * coefficient
    excess_imag = taper_rows * (spectrum_imag - band_imag) * coefficient
    basis_table = jnp.concatenate([cosine, -sine_table], axis=0)
    low_band = jnp.dot(jnp.concatenate([excess_real, excess_imag], axis=1), basis_table, precision=highest)
    return (band_rows + low_band).reshape(high_band.shape)
```

```python
import functools
import math

import jax
import jax.numpy as jnp
import numpy as np
from jax import lax
from jax.experimental import pallas as pl
from jax.experimental.pallas import tpu as pltpu
from jax.sharding import PartitionSpec as P

taper_width = 8.0
MESH = pl.DeviceIdType.MESH
VMEM = pltpu.VMEM
SMEM = pltpu.SMEM


def column_bins(bins_here):
    half = bins_here // 2
    column = np.arange(2 * bins_here)
    return (column // bins_here) * half + column % half, (column // half) % 2


def basis_tables(bins_here, parts, samples):
    bins, imaginary = column_bins(bins_here)
    time = np.arange(samples)[:, None]
    tables = []
    for part in range(parts):
        angle = ((part * bins_here + bins)[None, :] * time % samples) * (2.0 * math.pi / samples)
        tables.append(np.where(imaginary[None, :] == 1, -np.sin(angle), np.cos(angle)))
    exact = np.stack(tables)
    upper = exact.astype(jnp.bfloat16)
    lower = (exact - upper.astype(np.float64)).astype(jnp.bfloat16)
    return np.stack([upper, lower], axis=1)


def wide_dot(rows, upper, lower, dims):
    head = rows.astype(jnp.bfloat16)
    tail = (rows - head.astype(jnp.float32)).astype(jnp.bfloat16)
    dot = functools.partial(
        lax.dot_general, dimension_numbers=(dims, ((), ())), preferred_element_type=jnp.float32
    )
    return dot(head, upper) + (dot(head, lower) + dot(tail, upper))


def greet(peers):
    barrier = pltpu.get_barrier_semaphore()
    for peer in peers:
        pl.semaphore_signal(barrier, inc=1, device_id=peer, device_id_type=MESH)
    pl.semaphore_wait(barrier, len(peers))


def others(me, count):
    return [{"pt": lax.rem(me + step, count)} for step in range(1, count)]


def gather_kernel(
    count,
    strain_ref,
    scale_ref,
    mechanism_ref,
    slip_ref,
    onset_ref,
    band_ref,
    table_hbm,
    weights_ref,
    slips_ref,
    onsets_ref,
    spectrum_ref,
    strain_buf,
    wide_buf,
    table_buf,
    band_send,
    band_peer,
    local_sem,
    strain_sem,
    send_sem,
    recv_sem,
):
    me = lax.axis_index("pt")
    part = lax.axis_index("cmp")
    partner = {"cmp": 1 - part}
    blocks_here = scale_ref.shape[0]
    block = strain_ref.shape[0] // blocks_here
    bins = strain_ref.shape[2]
    half = bins // 2
    own = band_ref.shape[3]
    variations = band_ref.shape[1]
    strain_copies = []
    for b in range(blocks_here):
        rows = pl.ds(b * block, block)
        copy = pltpu.make_async_copy(strain_ref.at[rows], strain_buf.at[rows], strain_sem.at[b])
        copy.start()
        strain_copies.append(copy)
    table_copy = pltpu.make_async_copy(table_hbm.at[part], table_buf, local_sem.at[2])
    table_copy.start()
    keep = [
        pltpu.make_async_copy(slip_ref, slips_ref.at[pl.ds(me, 1)], local_sem.at[0]),
        pltpu.make_async_copy(onset_ref, onsets_ref.at[pl.ds(me, 1)], local_sem.at[1]),
    ]
    for copy in keep:
        copy.start()
    for c in range(2):
        band_send[pl.ds(c * variations, variations), :] = band_ref[0, :, c, :]
    greet(others(me, count) + [partner])
    sends = []
    for step, peer in enumerate(others(me, count)):
        for which, (source, target) in enumerate(((onset_ref, onsets_ref), (slip_ref, slips_ref))):
            copy = pltpu.make_async_remote_copy(
                src_ref=source,
                dst_ref=target.at[pl.ds(me, 1)],
                send_sem=send_sem.at[2 * step + which],
                recv_sem=recv_sem.at[2 * step + which],
                device_id=peer,
                device_id_type=MESH,
            )
            copy.start()
            sends.append(copy)
    band_copy = pltpu.make_async_remote_copy(
        src_ref=band_send,
        dst_ref=band_peer,
        send_sem=send_sem.at[2 * (count - 1)],
        recv_sem=recv_sem.at[2 * (count - 1)],
        device_id=partner,
        device_id_type=MESH,
    )
    band_copy.start()

    low_lanes = lax.broadcasted_iota(jnp.int32, (block, bins), 1) < half
    for b in range(blocks_here):
        strain_copies[b].wait()
        wide_buf[...] = (
            strain_buf[pl.ds(b * block, block)].astype(jnp.float32).reshape(block * 24, bins)
        )
        moment = mechanism_ref[:, pl.ds(b * block, block)]
        factors = jnp.transpose(jnp.concatenate([moment] * 4, axis=0)) * scale_ref[pl.ds(b, 1), :]
        for c in range(2):
            green = []
            for ri in range(2):
                total = None
                for j in range(6):
                    row = 12 * ri + 6 * c + j
                    term = factors[:, row : row + 1] * wide_buf[pl.ds(row, block, stride=24), :]
                    total = term if total is None else total + term
                green.append(total)
            real, imag = green
            real_turned = pltpu.roll(real, half, 1)
            imag_turned = pltpu.roll(imag, half, 1)
            lanes = pl.ds(c * bins, bins)
            pieces = (
                (0, 0, real, imag_turned),
                (0, 1, imag, -real_turned),
                (1, 0, real_turned, imag),
                (1, 1, imag_turned, -real),
            )
            for which, lower, first, second in pieces:
                weights_ref[b, which, pl.ds(lower * block, block), lanes] = jnp.where(
                    low_lanes, first, second
                ).astype(jnp.bfloat16)

    table_copy.wait()
    band_copy.wait()
    mine = pl.ds(pl.multiple_of(part * own, own), own)
    theirs = pl.ds(pl.multiple_of((1 - part) * own, own), own)
    down = ((1,), (0,))
    spectrum_ref[...] = wide_dot(
        band_send[...], table_buf[0, mine, :], table_buf[1, mine, :], down
    ) + wide_dot(band_peer[...], table_buf[0, theirs, :], table_buf[1, theirs, :], down)
    for copy in keep:
        copy.wait()
    for copy in sends:
        copy.wait()


def turn(first, second):
    return (
        first[0] * second[0] - first[1] * second[1],
        first[0] * second[1] + first[1] * second[0],
    )


def pair_kernel(
    step_angle,
    row_ref,
    blocks_ref,
    covered_ref,
    weights_ref,
    slips_ref,
    onsets_ref,
    partial_ref,
    total_ref,
):
    me = lax.axis_index("pt")
    part = lax.axis_index("cmp")
    blocks_here, halves, depth, columns = weights_ref.shape
    rows, variations, unused = slips_ref.shape
    block = depth // 2
    bins = columns // 2
    half = bins // 2
    fine_total = 16
    lowest = me * blocks_here
    lane_bin = lax.broadcasted_iota(jnp.int32, (variations, columns), 1) % half

    def one_row(row, carry):
        rupture = row_ref[row]
        total_ref[...] = jnp.zeros_like(total_ref)

        def one_slot(slot, carry):
            local = blocks_ref[rupture, slot] - lowest

            @pl.when((local >= 0) & (local < blocks_here))
            def _():
                lanes = pl.ds(pl.multiple_of(slot * block, block), block)
                angle = onsets_ref[row, :, lanes] * step_angle
                amplitude = slips_ref[row, :, lanes].astype(jnp.float32)
                powers = [None, (jnp.cos(angle), jnp.sin(angle))]
                for k in range(2, fine_total + 1):
                    powers.append(turn(powers[k // 2], powers[k - k // 2]))
                leap = powers[fine_total]
                far = leap
                for unused in range(int(math.log2(bins // fine_total))):
                    far = turn(far, far)
                second_part = part == 1
                coarse = (
                    amplitude * jnp.where(second_part, far[0], 1.0),
                    amplitude * jnp.where(second_part, far[1], 0.0),
                )
                per_half = half // fine_total
                for which in range(halves):
                    found = jnp.zeros((variations, columns), jnp.float32)
                    for h in range(per_half):
                        pieces = []
                        for k in range(fine_total):
                            phase = coarse if k == 0 else turn(coarse, powers[k])
                            pieces.append(
                                jnp.concatenate(
                                    [phase[0].astype(jnp.bfloat16), phase[1].astype(jnp.bfloat16)],
                                    axis=1,
                                )
                            )
                        product = jnp.dot(
                            jnp.concatenate(pieces, axis=0),
                            weights_ref[local, which],
                            preferred_element_type=jnp.float32,
                        )
                        for k in range(fine_total):
                            found = jnp.where(
                                lane_bin == h * fine_total + k,
                                product[k * variations : (k + 1) * variations],
                                found,
                            )
                        coarse = turn(coarse, leap)
                    total_ref[which] += found

            return carry

        lax.fori_loop(0, covered_ref[rupture], one_slot, 0)
        partial_ref[row] = total_ref[...].astype(jnp.bfloat16)
        return carry

    lax.fori_loop(0, rows, one_row, 0)


def merge_kernel(
    count,
    row_ref,
    crossover_ref,
    partial_ref,
    spectrum_ref,
    band_ref,
    table_hbm,
    out_ref,
    arrived,
    table_buf,
    low_send,
    low_peer,
    local_sem,
    send_sem,
    recv_sem,
):
    me = lax.axis_index("pt")
    part = lax.axis_index("cmp")
    partner = {"cmp": 1 - part}
    own = band_ref.shape[3]
    bins = partial_ref.shape[3] // 2
    half = bins // 2
    variations = partial_ref.shape[2]
    table_copy = pltpu.make_async_copy(table_hbm.at[part], table_buf, local_sem)
    table_copy.start()
    greet(others(me, count) + [partner])
    sends = []
    for step, peer in enumerate(others(me, count)):
        copy = pltpu.make_async_remote_copy(
            src_ref=partial_ref.at[peer["pt"]],
            dst_ref=arrived.at[step],
            send_sem=send_sem.at[step],
            recv_sem=recv_sem.at[step],
            device_id=peer,
            device_id_type=MESH,
        )
        copy.start()
        sends.append(copy)
    crossing = crossover_ref[row_ref[me]].astype(jnp.float32)
    column = lax.broadcasted_iota(jnp.int32, (variations, 2 * bins), 1)
    frequency_id = part * bins + (column // bins) * half + column % half
    frequency = frequency_id.astype(jnp.float32)
    taper = jnp.clip((crossing - frequency) / taper_width + 0.5, 0.0, 1.0)
    weight = taper * jnp.where(frequency_id == 0, 1.0, 2.0) / table_buf.shape[1]
    table_copy.wait()
    total = partial_ref[me].astype(jnp.float32)
    for step, copy in enumerate(sends):
        copy.wait()
        total = total + arrived[step].astype(jnp.float32)
    excess = []
    for c in range(2):
        lanes = slice(c * bins, (c + 1) * bins)
        spectrum = jnp.concatenate([total[0][:, lanes], total[1][:, lanes]], axis=1)
        here = pl.ds(c * variations, variations)
        excess.append((spectrum - spectrum_ref[here, :]) * weight)
    rows = jnp.concatenate(excess, axis=0)
    mine = pl.ds(pl.multiple_of(part * own, own), own)
    theirs = pl.ds(pl.multiple_of((1 - part) * own, own), own)
    across = ((1,), (1,))
    low_send[...] = wide_dot(rows, table_buf[0, theirs, :], table_buf[1, theirs, :], across)
    exchange = pltpu.make_async_remote_copy(
        src_ref=low_send,
        dst_ref=low_peer,
        send_sem=send_sem.at[count - 1],
        recv_sem=recv_sem.at[count - 1],
        device_id=partner,
        device_id_type=MESH,
    )
    exchange.start()
    low = wide_dot(rows, table_buf[0, mine, :], table_buf[1, mine, :], across)
    exchange.wait()
    low = low + low_peer[...]
    for c in range(2):
        out_ref[0, :, c, :] = band_ref[0, :, c, :] + low[c * variations : (c + 1) * variations]


def body(
    strain_green,
    green_scale,
    mechanism,
    slip_amplitude,
    onset_time,
    rupture_row,
    rupture_blocks,
    block_count,
    crossover,
    high_band,
):
    points, unused, bins = strain_green.shape
    blocks_here = green_scale.shape[0]
    block = points // blocks_here
    rows_here, variations, slots = slip_amplitude.shape
    count = lax.axis_size("pt")
    parts = lax.axis_size("cmp")
    own = high_band.shape[3]
    samples = own * parts
    rows = rows_here * count
    tables = jnp.asarray(basis_tables(bins, parts, samples))
    vmem = pl.BlockSpec(memory_space=VMEM)
    smem = pl.BlockSpec(memory_space=SMEM)
    anywhere = pl.BlockSpec(memory_space=pl.ANY)
    copies = 2 * (count - 1) + 1
    weights, slips, onsets, band_spectrum = pl.pallas_call(
        functools.partial(gather_kernel, count),
        out_shape=(
            jax.ShapeDtypeStruct((blocks_here, 2, 2 * block, 2 * bins), jnp.bfloat16),
            jax.ShapeDtypeStruct((rows, variations, slots), slip_amplitude.dtype),
            jax.ShapeDtypeStruct((rows, variations, slots), onset_time.dtype),
            jax.ShapeDtypeStruct((2 * variations, 2 * bins), jnp.float32),
        ),
        in_specs=[anywhere, vmem, vmem, vmem, vmem, vmem, anywhere],
        out_specs=(vmem, anywhere, anywhere, vmem),
        scratch_shapes=[
            VMEM(strain_green.shape, strain_green.dtype),
            VMEM((block * 24, bins), jnp.float32),
            VMEM((2, samples, 2 * bins), jnp.bfloat16),
            VMEM((2 * variations, own), jnp.float32),
            VMEM((2 * variations, own), jnp.float32),
            pltpu.SemaphoreType.DMA((3,)),
            pltpu.SemaphoreType.DMA((blocks_here,)),
            pltpu.SemaphoreType.DMA((copies,)),
            pltpu.SemaphoreType.DMA((copies,)),
        ],
        compiler_params=pltpu.CompilerParams(collective_id=0, has_side_effects=True),
        name="gather",
    )(strain_green, green_scale, mechanism, slip_amplitude, onset_time, high_band, tables)
    partial_spectra = pl.pallas_call(
        functools.partial(pair_kernel, 2.0 * math.pi / samples),
        out_shape=jax.ShapeDtypeStruct((rows, 2, variations, 2 * bins), jnp.bfloat16),
        in_specs=[smem, smem, smem, vmem, vmem, vmem],
        out_specs=vmem,
        scratch_shapes=[VMEM((2, variations, 2 * bins), jnp.float32)],
        name="pairs",
    )(rupture_row, rupture_blocks, block_count, weights, slips, onsets)
    return pl.pallas_call(
        functools.partial(merge_kernel, count),
        out_shape=jax.ShapeDtypeStruct(high_band.shape, high_band.dtype),
        in_specs=[smem, smem, vmem, vmem, vmem, anywhere],
        out_specs=vmem,
        scratch_shapes=[
            VMEM((count - 1, 2, variations, 2 * bins), jnp.bfloat16),
            VMEM((2, samples, 2 * bins), jnp.bfloat16),
            VMEM((2 * variations, own), jnp.float32),
            VMEM((2 * variations, own), jnp.float32),
            pltpu.SemaphoreType.DMA(()),
            pltpu.SemaphoreType.DMA((count,)),
            pltpu.SemaphoreType.DMA((count,)),
        ],
        compiler_params=pltpu.CompilerParams(collective_id=1, has_side_effects=True),
        name="merge",
    )(rupture_row, crossover, partial_spectra, band_spectrum, high_band, tables)


def solution(mesh):
    return jax.shard_map(
        body,
        mesh=mesh,
        in_specs=(
            P(("site", "pt"), None, "cmp"),
            P(("site", "pt"), None),
            P(None, "pt"),
            P("pt", "var", None),
            P("pt", "var", None),
            P(),
            P(),
            P(),
            P(),
            P(("site", "pt"), "var", None, "cmp"),
        ),
        out_specs=P(("site", "pt"), "var", None, "cmp"),
        check_vma=False,
    )
```

```python
import functools
import math

import jax
import jax.numpy as jnp
import numpy as np
from jax import lax
from jax.experimental import pallas as pl
from jax.experimental.pallas import tpu as pltpu
from jax.sharding import PartitionSpec as P

taper_width = 8.0
MESH = pl.DeviceIdType.MESH
VMEM = pltpu.VMEM
SMEM = pltpu.SMEM


def column_bins(bins_here):
    half = bins_here // 2
    column = np.arange(2 * bins_here)
    return (column // bins_here) * half + column % half, (column // half) % 2


def basis_tables(bins_here, parts, samples):
    bins, imaginary = column_bins(bins_here)
    time = np.arange(samples)[:, None]
    tables = []
    for part in range(parts):
        angle = ((part * bins_here + bins)[None, :] * time % samples) * (2.0 * math.pi / samples)
        tables.append(np.where(imaginary[None, :] == 1, -np.sin(angle), np.cos(angle)))
    exact = np.stack(tables)
    upper = exact.astype(jnp.bfloat16)
    lower = (exact - upper.astype(np.float64)).astype(jnp.bfloat16)
    return np.stack([upper, lower], axis=1)


def wide_dot(rows, upper, lower, dims):
    head = rows.astype(jnp.bfloat16)
    tail = (rows - head.astype(jnp.float32)).astype(jnp.bfloat16)
    dot = functools.partial(
        lax.dot_general, dimension_numbers=(dims, ((), ())), preferred_element_type=jnp.float32
    )
    return dot(head, upper) + (dot(head, lower) + dot(tail, upper))


def hail(peers):
    barrier = pltpu.get_barrier_semaphore()
    for peer in peers:
        pl.semaphore_signal(barrier, inc=1, device_id=peer, device_id_type=MESH)


def await_all(peers):
    pl.semaphore_wait(pltpu.get_barrier_semaphore(), len(peers))


def greet(peers):
    hail(peers)
    await_all(peers)


def others(me, count):
    return [{"pt": lax.rem(me + step, count)} for step in range(1, count)]


def gather_kernel(
    count,
    row_ref,
    blocks_ref,
    covered_ref,
    strain_ref,
    scale_ref,
    mechanism_ref,
    slip_ref,
    onset_ref,
    band_ref,
    table_hbm,
    weights_ref,
    slips_ref,
    onsets_ref,
    spectrum_ref,
    strain_buf,
    wide_buf,
    table_buf,
    band_send,
    band_peer,
    slip_pack,
    onset_pack,
    local_sem,
    strain_sem,
    send_sem,
    recv_sem,
    pass_sem,
    passed_sem,
):
    me = lax.axis_index("pt")
    part = lax.axis_index("cmp")
    partner = {"cmp": 1 - part}
    blocks_here = scale_ref.shape[0]
    block = strain_ref.shape[0] // blocks_here
    bins = strain_ref.shape[2]
    half = bins // 2
    own = band_ref.shape[3]
    variations = band_ref.shape[1]
    strain_copies = []
    for b in range(blocks_here):
        rows = pl.ds(b * block, block)
        copy = pltpu.make_async_copy(strain_ref.at[rows], strain_buf.at[rows], strain_sem.at[b])
        copy.start()
        strain_copies.append(copy)
    table_copy = pltpu.make_async_copy(table_hbm.at[part], table_buf, local_sem)
    table_copy.start()
    for c in range(2):
        band_send[pl.ds(c * variations, variations), :] = band_ref[0, :, c, :]
    peers = others(me, count)
    hail(peers + [partner])
    rupture = row_ref[me]
    covered = covered_ref[rupture]
    spread = variations // 2
    first_part = part == 0

    slot_total = blocks_ref.shape[1]
    whole = [
        (
            onset_ref[0, :, slot * block : (slot + 1) * block],
            slip_ref[0, :, slot * block : (slot + 1) * block].astype(jnp.float32),
        )
        for slot in range(slot_total)
    ]
    halved = [
        tuple(jnp.where(first_part, tile[:spread], tile[spread:]) for tile in pair)
        for pair in whole
    ]

    def packed(target, tiles):
        lowest = target * blocks_here
        totals = [[jnp.zeros_like(tile) for tile in tiles[0]] for k in range(blocks_here)]
        found = jnp.int32(0)
        for slot in range(slot_total):
            named = blocks_ref[rupture, slot]
            live = (slot < covered) & (named >= lowest) & (named < lowest + blocks_here)
            for k in range(min(blocks_here, slot + 1)):
                share = (live & (found == k)).astype(jnp.int32).astype(jnp.float32)
                for which in range(2):
                    totals[k][which] = totals[k][which] + share * tiles[slot][which]
            found = found + live.astype(jnp.int32)
        return totals

    def pack(step, carry):
        for k, (onset, slip) in enumerate(packed(lax.rem(me + 1 + step, count), halved)):
            onset_pack[step, k] = onset
            slip_pack[step, k] = slip.astype(slip_pack.dtype)
        return carry

    lax.fori_loop(0, count - 1, pack, 0)
    await_all(peers + [partner])
    sends = []
    for step, peer in enumerate(peers):
        for which, (source, target) in enumerate(((onset_pack, onsets_ref), (slip_pack, slips_ref))):
            copy = pltpu.make_async_remote_copy(
                src_ref=source.at[step],
                dst_ref=target.at[me, part],
                send_sem=send_sem.at[2 * step + which],
                recv_sem=recv_sem.at[2 * step + which],
                device_id=peer,
                device_id_type=MESH,
            )
            copy.start()
            sends.append(copy)
    band_copy = pltpu.make_async_remote_copy(
        src_ref=band_send,
        dst_ref=band_peer,
        send_sem=send_sem.at[2 * (count - 1)],
        recv_sem=recv_sem.at[2 * (count - 1)],
        device_id=partner,
        device_id_type=MESH,
    )
    band_copy.start()
    for k, (onset, slip) in enumerate(packed(me, whole)):
        for h in range(2):
            slips_ref[me, h, k] = slip[h * spread : (h + 1) * spread].astype(slips_ref.dtype)
            onsets_ref[me, h, k] = onset[h * spread : (h + 1) * spread]

    low_lanes = lax.broadcasted_iota(jnp.int32, (block, bins), 1) < half
    for b in range(blocks_here):
        strain_copies[b].wait()
        wide_buf[...] = (
            strain_buf[pl.ds(b * block, block)].astype(jnp.float32).reshape(block * 24, bins)
        )
        moment = mechanism_ref[:, pl.ds(b * block, block)]
        factors = jnp.transpose(jnp.concatenate([moment] * 4, axis=0)) * scale_ref[pl.ds(b, 1), :]
        for c in range(2):
            green = []
            for ri in range(2):
                total = None
                for j in range(6):
                    row = 12 * ri + 6 * c + j
                    term = factors[:, row : row + 1] * wide_buf[pl.ds(row, block, stride=24), :]
                    total = term if total is None else total + term
                green.append(total)
            real, imag = green
            real_turned = pltpu.roll(real, half, 1)
            imag_turned = pltpu.roll(imag, half, 1)
            lanes = pl.ds(c * bins, bins)
            pieces = (
                (0, 0, real, imag_turned),
                (0, 1, imag, -real_turned),
                (1, 0, real_turned, imag),
                (1, 1, imag_turned, -real),
            )
            for which, lower, first, second in pieces:
                weights_ref[b, which, pl.ds(lower * block, block), lanes] = jnp.where(
                    low_lanes, first, second
                ).astype(jnp.bfloat16)

    passes = []
    for step in range(count - 1):
        source_row = lax.rem(me + count - 1 - step, count)
        for which, target in enumerate((onsets_ref, slips_ref)):
            sends[2 * step + which].wait_recv()
            held = target.at[source_row, part]
            copy = pltpu.make_async_remote_copy(
                src_ref=held,
                dst_ref=held,
                send_sem=pass_sem.at[2 * step + which],
                recv_sem=passed_sem.at[2 * step + which],
                device_id=partner,
                device_id_type=MESH,
            )
            copy.start()
            passes.append(copy)
    table_copy.wait()
    band_copy.wait()
    mine = pl.ds(pl.multiple_of(part * own, own), own)
    theirs = pl.ds(pl.multiple_of((1 - part) * own, own), own)
    down = ((1,), (0,))
    spectrum_ref[...] = wide_dot(
        band_send[...], table_buf[0, mine, :], table_buf[1, mine, :], down
    ) + wide_dot(band_peer[...], table_buf[0, theirs, :], table_buf[1, theirs, :], down)
    for copy in sends:
        copy.wait_send()
    for copy in passes:
        copy.wait()


def turn(first, second):
    return (
        first[0] * second[0] - first[1] * second[1],
        first[0] * second[1] + first[1] * second[0],
    )


def pair_kernel(
    step_angle,
    row_ref,
    blocks_ref,
    covered_ref,
    weights_ref,
    slips_ref,
    onsets_ref,
    partial_ref,
    total_ref,
):
    me = lax.axis_index("pt")
    part = lax.axis_index("cmp")
    blocks_here, halves, depth, columns = weights_ref.shape
    rows, shares, unused, spread, block = slips_ref.shape
    variations = shares * spread
    bins = columns // 2
    half = bins // 2
    fine_total = 16
    lowest = me * blocks_here
    lane_bin = lax.broadcasted_iota(jnp.int32, (variations, columns), 1) % half

    def one_row(row, carry):
        rupture = row_ref[row]
        total_ref[...] = jnp.zeros_like(total_ref)

        def one_slot(slot, found_here):
            local = blocks_ref[rupture, slot] - lowest
            live = (local >= 0) & (local < blocks_here)

            @pl.when(live)
            def _():
                angle = step_angle * jnp.concatenate(
                    [onsets_ref[row, h, found_here] for h in range(shares)], axis=0
                )
                amplitude = jnp.concatenate(
                    [slips_ref[row, h, found_here].astype(jnp.float32) for h in range(shares)],
                    axis=0,
                )
                powers = [None, (jnp.cos(angle), jnp.sin(angle))]
                for k in range(2, fine_total + 1):
                    powers.append(turn(powers[k // 2], powers[k - k // 2]))
                leap = powers[fine_total]
                far = leap
                for unused in range(int(math.log2(bins // fine_total))):
                    far = turn(far, far)
                second_part = part == 1
                coarse = (
                    amplitude * jnp.where(second_part, far[0], 1.0),
                    amplitude * jnp.where(second_part, far[1], 0.0),
                )
                per_half = half // fine_total
                for which in range(halves):
                    found = jnp.zeros((variations, columns), jnp.float32)
                    for h in range(per_half):
                        pieces = []
                        for k in range(fine_total):
                            phase = coarse if k == 0 else turn(coarse, powers[k])
                            pieces.append(
                                jnp.concatenate(
                                    [phase[0].astype(jnp.bfloat16), phase[1].astype(jnp.bfloat16)],
                                    axis=1,
                                )
                            )
                        product = jnp.dot(
                            jnp.concatenate(pieces, axis=0),
                            weights_ref[local, which],
                            preferred_element_type=jnp.float32,
                        )
                        for k in range(fine_total):
                            found = jnp.where(
                                lane_bin == h * fine_total + k,
                                product[k * variations : (k + 1) * variations],
                                found,
                            )
                        coarse = turn(coarse, leap)
                    total_ref[which] += found

            return found_here + live.astype(jnp.int32)

        lax.fori_loop(0, covered_ref[rupture], one_slot, jnp.int32(0))
        partial_ref[row] = total_ref[...].astype(jnp.bfloat16)
        return carry

    lax.fori_loop(0, rows, one_row, 0)


def merge_kernel(
    count,
    row_ref,
    crossover_ref,
    partial_ref,
    spectrum_ref,
    band_ref,
    table_hbm,
    out_ref,
    arrived,
    table_buf,
    low_send,
    low_peer,
    local_sem,
    send_sem,
    recv_sem,
):
    me = lax.axis_index("pt")
    part = lax.axis_index("cmp")
    partner = {"cmp": 1 - part}
    own = band_ref.shape[3]
    bins = partial_ref.shape[3] // 2
    half = bins // 2
    variations = partial_ref.shape[2]
    table_copy = pltpu.make_async_copy(table_hbm.at[part], table_buf, local_sem)
    table_copy.start()
    greet(others(me, count) + [partner])
    sends = []
    for step, peer in enumerate(others(me, count)):
        copy = pltpu.make_async_remote_copy(
            src_ref=partial_ref.at[peer["pt"]],
            dst_ref=arrived.at[step],
            send_sem=send_sem.at[step],
            recv_sem=recv_sem.at[step],
            device_id=peer,
            device_id_type=MESH,
        )
        copy.start()
        sends.append(copy)
    crossing = crossover_ref[row_ref[me]].astype(jnp.float32)
    column = lax.broadcasted_iota(jnp.int32, (variations, 2 * bins), 1)
    frequency_id = part * bins + (column // bins) * half + column % half
    frequency = frequency_id.astype(jnp.float32)
    taper = jnp.clip((crossing - frequency) / taper_width + 0.5, 0.0, 1.0)
    weight = taper * jnp.where(frequency_id == 0, 1.0, 2.0) / table_buf.shape[1]
    table_copy.wait()
    total = partial_ref[me].astype(jnp.float32)
    for step, copy in enumerate(sends):
        copy.wait()
        total = total + arrived[step].astype(jnp.float32)
    excess = []
    for c in range(2):
        lanes = slice(c * bins, (c + 1) * bins)
        spectrum = jnp.concatenate([total[0][:, lanes], total[1][:, lanes]], axis=1)
        here = pl.ds(c * variations, variations)
        excess.append((spectrum - spectrum_ref[here, :]) * weight)
    rows = jnp.concatenate(excess, axis=0)
    mine = pl.ds(pl.multiple_of(part * own, own), own)
    theirs = pl.ds(pl.multiple_of((1 - part) * own, own), own)
    across = ((1,), (1,))
    low_send[...] = wide_dot(rows, table_buf[0, theirs, :], table_buf[1, theirs, :], across)
    exchange = pltpu.make_async_remote_copy(
        src_ref=low_send,
        dst_ref=low_peer,
        send_sem=send_sem.at[count - 1],
        recv_sem=recv_sem.at[count - 1],
        device_id=partner,
        device_id_type=MESH,
    )
    exchange.start()
    low = wide_dot(rows, table_buf[0, mine, :], table_buf[1, mine, :], across)
    exchange.wait()
    low = low + low_peer[...]
    for c in range(2):
        out_ref[0, :, c, :] = band_ref[0, :, c, :] + low[c * variations : (c + 1) * variations]


def body(
    strain_green,
    green_scale,
    mechanism,
    slip_amplitude,
    onset_time,
    rupture_row,
    rupture_blocks,
    block_count,
    crossover,
    high_band,
):
    points, unused, bins = strain_green.shape
    blocks_here = green_scale.shape[0]
    block = points // blocks_here
    rows_here, variations, slots = slip_amplitude.shape
    count = lax.axis_size("pt")
    parts = lax.axis_size("cmp")
    own = high_band.shape[3]
    samples = own * parts
    rows = rows_here * count
    tables = jnp.asarray(basis_tables(bins, parts, samples))
    vmem = pl.BlockSpec(memory_space=VMEM)
    smem = pl.BlockSpec(memory_space=SMEM)
    anywhere = pl.BlockSpec(memory_space=pl.ANY)
    copies = 2 * (count - 1) + 1
    share = (blocks_here, variations // 2, block)
    weights, slips, onsets, band_spectrum = pl.pallas_call(
        functools.partial(gather_kernel, count),
        out_shape=(
            jax.ShapeDtypeStruct((blocks_here, 2, 2 * block, 2 * bins), jnp.bfloat16),
            jax.ShapeDtypeStruct((rows, 2) + share, slip_amplitude.dtype),
            jax.ShapeDtypeStruct((rows, 2) + share, onset_time.dtype),
            jax.ShapeDtypeStruct((2 * variations, 2 * bins), jnp.float32),
        ),
        in_specs=[smem, smem, smem, anywhere, vmem, vmem, vmem, vmem, vmem, anywhere],
        out_specs=(vmem, vmem, vmem, vmem),
        scratch_shapes=[
            VMEM(strain_green.shape, strain_green.dtype),
            VMEM((block * 24, bins), jnp.float32),
            VMEM((2, samples, 2 * bins), jnp.bfloat16),
            VMEM((2 * variations, own), jnp.float32),
            VMEM((2 * variations, own), jnp.float32),
            VMEM((count - 1,) + share, slip_amplitude.dtype),
            VMEM((count - 1,) + share, onset_time.dtype),
            pltpu.SemaphoreType.DMA(()),
            pltpu.SemaphoreType.DMA((blocks_here,)),
            pltpu.SemaphoreType.DMA((copies,)),
            pltpu.SemaphoreType.DMA((copies,)),
            pltpu.SemaphoreType.DMA((copies - 1,)),
            pltpu.SemaphoreType.DMA((copies - 1,)),
        ],
        compiler_params=pltpu.CompilerParams(collective_id=0, has_side_effects=True),
        name="gather",
    )(
        rupture_row,
        rupture_blocks,
        block_count,
        strain_green,
        green_scale,
        mechanism,
        slip_amplitude,
        onset_time,
        high_band,
        tables,
    )
    partial_spectra = pl.pallas_call(
        functools.partial(pair_kernel, 2.0 * math.pi / samples),
        out_shape=jax.ShapeDtypeStruct((rows, 2, variations, 2 * bins), jnp.bfloat16),
        in_specs=[smem, smem, smem, vmem, vmem, vmem],
        out_specs=vmem,
        scratch_shapes=[VMEM((2, variations, 2 * bins), jnp.float32)],
        name="pairs",
    )(rupture_row, rupture_blocks, block_count, weights, slips, onsets)
    return pl.pallas_call(
        functools.partial(merge_kernel, count),
        out_shape=jax.ShapeDtypeStruct(high_band.shape, high_band.dtype),
        in_specs=[smem, smem, vmem, vmem, vmem, anywhere],
        out_specs=vmem,
        scratch_shapes=[
            VMEM((count - 1, 2, variations, 2 * bins), jnp.bfloat16),
            VMEM((2, samples, 2 * bins), jnp.bfloat16),
            VMEM((2 * variations, own), jnp.float32),
            VMEM((2 * variations, own), jnp.float32),
            pltpu.SemaphoreType.DMA(()),
            pltpu.SemaphoreType.DMA((count,)),
            pltpu.SemaphoreType.DMA((count,)),
        ],
        compiler_params=pltpu.CompilerParams(collective_id=1, has_side_effects=True),
        name="merge",
    )(rupture_row, crossover, partial_spectra, band_spectrum, high_band, tables)


def solution(mesh):
    return jax.shard_map(
        body,
        mesh=mesh,
        in_specs=(
            P(("site", "pt"), None, "cmp"),
            P(("site", "pt"), None),
            P(None, "pt"),
            P("pt", "var", None),
            P("pt", "var", None),
            P(),
            P(),
            P(),
            P(),
            P(("site", "pt"), "var", None, "cmp"),
        ),
        out_specs=P(("site", "pt"), "var", None, "cmp"),
        check_vma=False,
    )
```

```python
import functools
import math

import jax
import jax.numpy as jnp
import numpy as np
from jax import lax
from jax.experimental import pallas as pl
from jax.experimental.pallas import tpu as pltpu
from jax.sharding import PartitionSpec as P

taper_width = 8.0
MESH = pl.DeviceIdType.MESH
VMEM = pltpu.VMEM
SMEM = pltpu.SMEM


def column_bins(bins_here):
    half = bins_here // 2
    column = np.arange(2 * bins_here)
    return (column // bins_here) * half + column % half, (column // half) % 2


def basis_tables(bins_here, parts, samples):
    bins, imaginary = column_bins(bins_here)
    time = np.arange(samples)[:, None]
    tables = []
    for part in range(parts):
        angle = ((part * bins_here + bins)[None, :] * time % samples) * (2.0 * math.pi / samples)
        tables.append(np.where(imaginary[None, :] == 1, -np.sin(angle), np.cos(angle)))
    exact = np.stack(tables)
    upper = exact.astype(jnp.bfloat16)
    lower = (exact - upper.astype(np.float64)).astype(jnp.bfloat16)
    return np.stack([upper, lower], axis=1)


def wide_dot(rows, upper, lower, dims):
    head = rows.astype(jnp.bfloat16)
    tail = (rows - head.astype(jnp.float32)).astype(jnp.bfloat16)
    dot = functools.partial(
        lax.dot_general, dimension_numbers=(dims, ((), ())), preferred_element_type=jnp.float32
    )
    return dot(head, upper) + (dot(head, lower) + dot(tail, upper))


def hail(peers):
    barrier = pltpu.get_barrier_semaphore()
    for peer in peers:
        pl.semaphore_signal(barrier, inc=1, device_id=peer, device_id_type=MESH)


def await_all(peers):
    pl.semaphore_wait(pltpu.get_barrier_semaphore(), len(peers))


def greet(peers):
    hail(peers)
    await_all(peers)


def others(me, count):
    return [{"pt": lax.rem(me + step, count)} for step in range(1, count)]


def gather_kernel(
    count,
    row_ref,
    blocks_ref,
    covered_ref,
    strain_ref,
    scale_ref,
    mechanism_ref,
    slip_ref,
    onset_ref,
    band_ref,
    table_hbm,
    weights_ref,
    slips_ref,
    onsets_ref,
    spectrum_ref,
    band_send,
    final_table,
    strain_buf,
    wide_buf,
    table_buf,
    band_peer,
    slip_pack,
    onset_pack,
    local_sem,
    strain_sem,
    send_sem,
    recv_sem,
    pass_sem,
    passed_sem,
):
    me = lax.axis_index("pt")
    part = lax.axis_index("cmp")
    partner = {"cmp": 1 - part}
    blocks_here = scale_ref.shape[0]
    block = strain_ref.shape[0] // blocks_here
    bins = strain_ref.shape[2]
    half = bins // 2
    own = band_ref.shape[3]
    variations = band_ref.shape[1]
    strain_copies = []
    for b in range(blocks_here):
        rows = pl.ds(b * block, block)
        copy = pltpu.make_async_copy(strain_ref.at[rows], strain_buf.at[rows], strain_sem.at[b])
        copy.start()
        strain_copies.append(copy)
    table_copy = pltpu.make_async_copy(table_hbm.at[part], table_buf, local_sem.at[0])
    table_copy.start()
    mine = pl.ds(pl.multiple_of(part * own, own), own)
    theirs = pl.ds(pl.multiple_of((1 - part) * own, own), own)
    final_copies = []
    for p in range(final_table.shape[0]):
        for which in range(2):
            copy = pltpu.make_async_copy(
                table_hbm.at[p, which, mine], final_table.at[p, which], local_sem.at[1 + 2 * p + which]
            )
            copy.start()
            final_copies.append(copy)
    for c in range(2):
        band_send[pl.ds(c * variations, variations), :] = band_ref[0, :, c, :]
    peers = others(me, count)
    hail(peers + [partner])
    rupture = row_ref[me]
    covered = covered_ref[rupture]
    spread = variations // 2
    first_part = part == 0

    slot_total = blocks_ref.shape[1]
    whole = [
        (
            onset_ref[0, :, slot * block : (slot + 1) * block],
            slip_ref[0, :, slot * block : (slot + 1) * block].astype(jnp.float32),
        )
        for slot in range(slot_total)
    ]
    halved = [
        tuple(jnp.where(first_part, tile[:spread], tile[spread:]) for tile in pair)
        for pair in whole
    ]

    def packed(target, tiles):
        lowest = target * blocks_here
        totals = [[jnp.zeros_like(tile) for tile in tiles[0]] for k in range(blocks_here)]
        found = jnp.int32(0)
        for slot in range(slot_total):
            named = blocks_ref[rupture, slot]
            live = (slot < covered) & (named >= lowest) & (named < lowest + blocks_here)
            for k in range(min(blocks_here, slot + 1)):
                share = (live & (found == k)).astype(jnp.int32).astype(jnp.float32)
                for which in range(2):
                    totals[k][which] = totals[k][which] + share * tiles[slot][which]
            found = found + live.astype(jnp.int32)
        return totals

    def pack(step, carry):
        for k, (onset, slip) in enumerate(packed(lax.rem(me + 1 + step, count), halved)):
            onset_pack[step, k] = onset
            slip_pack[step, k] = slip.astype(slip_pack.dtype)
        return carry

    lax.fori_loop(0, count - 1, pack, 0)
    await_all(peers + [partner])
    sends = []
    for step, peer in enumerate(peers):
        for which, (source, target) in enumerate(((onset_pack, onsets_ref), (slip_pack, slips_ref))):
            copy = pltpu.make_async_remote_copy(
                src_ref=source.at[step],
                dst_ref=target.at[me, part],
                send_sem=send_sem.at[2 * step + which],
                recv_sem=recv_sem.at[2 * step + which],
                device_id=peer,
                device_id_type=MESH,
            )
            copy.start()
            sends.append(copy)
    band_copy = pltpu.make_async_remote_copy(
        src_ref=band_send,
        dst_ref=band_peer,
        send_sem=send_sem.at[2 * (count - 1)],
        recv_sem=recv_sem.at[2 * (count - 1)],
        device_id=partner,
        device_id_type=MESH,
    )
    band_copy.start()
    for k, (onset, slip) in enumerate(packed(me, whole)):
        for h in range(2):
            slips_ref[me, h, k] = slip[h * spread : (h + 1) * spread].astype(slips_ref.dtype)
            onsets_ref[me, h, k] = onset[h * spread : (h + 1) * spread]

    low_lanes = lax.broadcasted_iota(jnp.int32, (block, bins), 1) < half
    for b in range(blocks_here):
        strain_copies[b].wait()
        wide_buf[...] = (
            strain_buf[pl.ds(b * block, block)].astype(jnp.float32).reshape(block * 24, bins)
        )
        moment = mechanism_ref[:, pl.ds(b * block, block)]
        factors = jnp.transpose(jnp.concatenate([moment] * 4, axis=0)) * scale_ref[pl.ds(b, 1), :]
        for c in range(2):
            green = []
            for ri in range(2):
                total = None
                for j in range(6):
                    row = 12 * ri + 6 * c + j
                    term = factors[:, row : row + 1] * wide_buf[pl.ds(row, block, stride=24), :]
                    total = term if total is None else total + term
                green.append(total)
            real, imag = green
            real_turned = pltpu.roll(real, half, 1)
            imag_turned = pltpu.roll(imag, half, 1)
            lanes = pl.ds(c * bins, bins)
            pieces = (
                (0, 0, real, imag_turned),
                (0, 1, imag, -real_turned),
                (1, 0, real_turned, imag),
                (1, 1, imag_turned, -real),
            )
            for which, lower, first, second in pieces:
                weights_ref[b, which, pl.ds(lower * block, block), lanes] = jnp.where(
                    low_lanes, first, second
                ).astype(jnp.bfloat16)

    passes = []
    for step in range(count - 1):
        source_row = lax.rem(me + count - 1 - step, count)
        for which, target in enumerate((onsets_ref, slips_ref)):
            sends[2 * step + which].wait_recv()
            held = target.at[source_row, part]
            copy = pltpu.make_async_remote_copy(
                src_ref=held,
                dst_ref=held,
                send_sem=pass_sem.at[2 * step + which],
                recv_sem=passed_sem.at[2 * step + which],
                device_id=partner,
                device_id_type=MESH,
            )
            copy.start()
            passes.append(copy)
    table_copy.wait()
    band_copy.wait()
    down = ((1,), (0,))
    spectrum_ref[...] = wide_dot(
        band_send[...], table_buf[0, mine, :], table_buf[1, mine, :], down
    ) + wide_dot(band_peer[...], table_buf[0, theirs, :], table_buf[1, theirs, :], down)
    for copy in final_copies:
        copy.wait()
    for copy in sends:
        copy.wait_send()
    for copy in passes:
        copy.wait()


def turn(first, second):
    return (
        first[0] * second[0] - first[1] * second[1],
        first[0] * second[1] + first[1] * second[0],
    )


def pair_kernel(
    step_angle,
    row_ref,
    blocks_ref,
    covered_ref,
    weights_ref,
    slips_ref,
    onsets_ref,
    partial_ref,
    total_ref,
):
    me = lax.axis_index("pt")
    part = lax.axis_index("cmp")
    blocks_here, halves, depth, columns = weights_ref.shape
    rows, shares, unused, spread, block = slips_ref.shape
    variations = shares * spread
    bins = columns // 2
    half = bins // 2
    fine_total = 16
    lowest = me * blocks_here
    lane_bin = lax.broadcasted_iota(jnp.int32, (variations, columns), 1) % half

    def one_row(row, carry):
        rupture = row_ref[row]
        total_ref[...] = jnp.zeros_like(total_ref)

        def one_slot(slot, found_here):
            local = blocks_ref[rupture, slot] - lowest
            live = (local >= 0) & (local < blocks_here)

            @pl.when(live)
            def _():
                angle = step_angle * jnp.concatenate(
                    [onsets_ref[row, h, found_here] for h in range(shares)], axis=0
                )
                amplitude = jnp.concatenate(
                    [slips_ref[row, h, found_here].astype(jnp.float32) for h in range(shares)],
                    axis=0,
                )
                powers = [None, (jnp.cos(angle), jnp.sin(angle))]
                for k in range(2, fine_total + 1):
                    powers.append(turn(powers[k // 2], powers[k - k // 2]))
                leap = powers[fine_total]
                far = leap
                for unused in range(int(math.log2(bins // fine_total))):
                    far = turn(far, far)
                second_part = part == 1
                coarse = (
                    amplitude * jnp.where(second_part, far[0], 1.0),
                    amplitude * jnp.where(second_part, far[1], 0.0),
                )
                per_half = half // fine_total
                for which in range(halves):
                    found = jnp.zeros((variations, columns), jnp.float32)
                    for h in range(per_half):
                        pieces = []
                        for k in range(fine_total):
                            phase = coarse if k == 0 else turn(coarse, powers[k])
                            pieces.append(
                                jnp.concatenate(
                                    [phase[0].astype(jnp.bfloat16), phase[1].astype(jnp.bfloat16)],
                                    axis=1,
                                )
                            )
                        product = jnp.dot(
                            jnp.concatenate(pieces, axis=0),
                            weights_ref[local, which],
                            preferred_element_type=jnp.float32,
                        )
                        for k in range(fine_total):
                            found = jnp.where(
                                lane_bin == h * fine_total + k,
                                product[k * variations : (k + 1) * variations],
                                found,
                            )
                        coarse = turn(coarse, leap)
                    total_ref[which] += found

            return found_here + live.astype(jnp.int32)

        lax.fori_loop(0, covered_ref[rupture], one_slot, jnp.int32(0))
        partial_ref[row] = total_ref[...].astype(jnp.bfloat16)
        return carry

    lax.fori_loop(0, rows, one_row, 0)


def merge_kernel(
    count,
    samples,
    row_ref,
    crossover_ref,
    partial_ref,
    spectrum_ref,
    excess_ref,
    arrived,
    excess_send,
    send_sem,
    recv_sem,
):
    me = lax.axis_index("pt")
    part = lax.axis_index("cmp")
    partner = {"cmp": 1 - part}
    bins = partial_ref.shape[3] // 2
    half = bins // 2
    variations = partial_ref.shape[2]
    greet(others(me, count) + [partner])
    sends = []
    for step, peer in enumerate(others(me, count)):
        copy = pltpu.make_async_remote_copy(
            src_ref=partial_ref.at[peer["pt"]],
            dst_ref=arrived.at[step],
            send_sem=send_sem.at[step],
            recv_sem=recv_sem.at[step],
            device_id=peer,
            device_id_type=MESH,
        )
        copy.start()
        sends.append(copy)
    crossing = crossover_ref[row_ref[me]].astype(jnp.float32)
    column = lax.broadcasted_iota(jnp.int32, (variations, 2 * bins), 1)
    frequency_id = part * bins + (column // bins) * half + column % half
    frequency = frequency_id.astype(jnp.float32)
    taper = jnp.clip((crossing - frequency) / taper_width + 0.5, 0.0, 1.0)
    weight = taper * jnp.where(frequency_id == 0, 1.0, 2.0) / samples
    total = partial_ref[me].astype(jnp.float32)
    for step, copy in enumerate(sends):
        copy.wait_recv()
        total = total + arrived[step].astype(jnp.float32)
    for c in range(2):
        lanes = slice(c * bins, (c + 1) * bins)
        here = pl.ds(c * variations, variations)
        spectrum = jnp.concatenate([total[0][:, lanes], total[1][:, lanes]], axis=1)
        excess_send[here, :] = (spectrum - spectrum_ref[here, :]) * weight
    exchange = pltpu.make_async_remote_copy(
        src_ref=excess_send,
        dst_ref=excess_ref.at[1],
        send_sem=send_sem.at[count - 1],
        recv_sem=recv_sem.at[count - 1],
        device_id=partner,
        device_id_type=MESH,
    )
    exchange.start()
    excess_ref[0] = excess_send[...]
    for copy in sends:
        copy.wait_send()
    exchange.wait()


def final_kernel(excess_ref, band_ref, table_ref, out_ref):
    part = lax.axis_index("cmp")
    variations = out_ref.shape[1]
    across = ((1,), (1,))
    low = band_ref[...]
    for which in range(2):
        source = lax.rem(part + which, 2)
        low = low + wide_dot(
            excess_ref[which], table_ref[source, 0], table_ref[source, 1], across
        )
    for c in range(2):
        out_ref[0, :, c, :] = low[c * variations : (c + 1) * variations]


def stay(array):
    return pltpu.with_memory_space_constraint(array, VMEM)


def body(
    strain_green,
    green_scale,
    mechanism,
    slip_amplitude,
    onset_time,
    rupture_row,
    rupture_blocks,
    block_count,
    crossover,
    high_band,
):
    points, unused, bins = strain_green.shape
    blocks_here = green_scale.shape[0]
    block = points // blocks_here
    rows_here, variations, slots = slip_amplitude.shape
    count = lax.axis_size("pt")
    parts = lax.axis_size("cmp")
    own = high_band.shape[3]
    samples = own * parts
    rows = rows_here * count
    tables = jnp.asarray(basis_tables(bins, parts, samples))
    vmem = pl.BlockSpec(memory_space=VMEM)
    smem = pl.BlockSpec(memory_space=SMEM)
    anywhere = pl.BlockSpec(memory_space=pltpu.HBM)
    grant = 24 * 1024 * 1024
    copies = 2 * (count - 1) + 1
    share = (blocks_here, variations // 2, block)
    weights, slips, onsets, band_spectrum, band_rows, final_table = pl.pallas_call(
        functools.partial(gather_kernel, count),
        out_shape=(
            VMEM((blocks_here, 2, 2 * block, 2 * bins), jnp.bfloat16),
            VMEM((rows, 2) + share, slip_amplitude.dtype),
            VMEM((rows, 2) + share, onset_time.dtype),
            VMEM((2 * variations, 2 * bins), jnp.float32),
            VMEM((2 * variations, own), jnp.float32),
            VMEM((parts, 2, own, 2 * bins), jnp.bfloat16),
        ),
        in_specs=[smem, smem, smem, anywhere, vmem, vmem, vmem, vmem, vmem, anywhere],
        out_specs=(vmem,) * 6,
        scratch_shapes=[
            VMEM(strain_green.shape, strain_green.dtype),
            VMEM((block * 24, bins), jnp.float32),
            VMEM((2, samples, 2 * bins), jnp.bfloat16),
            VMEM((2 * variations, own), jnp.float32),
            VMEM((count - 1,) + share, slip_amplitude.dtype),
            VMEM((count - 1,) + share, onset_time.dtype),
            pltpu.SemaphoreType.DMA((1 + 2 * parts,)),
            pltpu.SemaphoreType.DMA((blocks_here,)),
            pltpu.SemaphoreType.DMA((copies,)),
            pltpu.SemaphoreType.DMA((copies,)),
            pltpu.SemaphoreType.DMA((copies - 1,)),
            pltpu.SemaphoreType.DMA((copies - 1,)),
        ],
        compiler_params=pltpu.CompilerParams(collective_id=0, has_side_effects=True),
        name="gather",
    )(
        rupture_row,
        rupture_blocks,
        block_count,
        strain_green,
        green_scale,
        mechanism,
        slip_amplitude,
        onset_time,
        high_band,
        tables,
    )
    partial_spectra = pl.pallas_call(
        functools.partial(pair_kernel, 2.0 * math.pi / samples),
        out_shape=VMEM((rows, 2, variations, 2 * bins), jnp.bfloat16),
        in_specs=[smem, smem, smem, vmem, vmem, vmem],
        out_specs=vmem,
        scratch_shapes=[VMEM((2, variations, 2 * bins), jnp.float32)],
        compiler_params=pltpu.CompilerParams(vmem_limit_bytes=grant),
        name="pairs",
    )(rupture_row, rupture_blocks, block_count, stay(weights), stay(slips), stay(onsets))
    excess = pl.pallas_call(
        functools.partial(merge_kernel, count, samples),
        out_shape=VMEM((2, 2 * variations, 2 * bins), jnp.float32),
        in_specs=[smem, smem, vmem, vmem],
        out_specs=vmem,
        scratch_shapes=[
            VMEM((count - 1, 2, variations, 2 * bins), jnp.bfloat16),
            VMEM((2 * variations, 2 * bins), jnp.float32),
            pltpu.SemaphoreType.DMA((count,)),
            pltpu.SemaphoreType.DMA((count,)),
        ],
        compiler_params=pltpu.CompilerParams(collective_id=1, has_side_effects=True, vmem_limit_bytes=grant),
        name="merge",
    )(rupture_row, crossover, stay(partial_spectra), stay(band_spectrum))
    return pl.pallas_call(
        final_kernel,
        out_shape=jax.ShapeDtypeStruct(high_band.shape, high_band.dtype),
        in_specs=[vmem, vmem, vmem],
        out_specs=vmem,
        compiler_params=pltpu.CompilerParams(vmem_limit_bytes=grant),
        name="final",
    )(stay(excess), stay(band_rows), stay(final_table))


def solution(mesh):
    return jax.shard_map(
        body,
        mesh=mesh,
        in_specs=(
            P(("site", "pt"), None, "cmp"),
            P(("site", "pt"), None),
            P(None, "pt"),
            P("pt", "var", None),
            P("pt", "var", None),
            P(),
            P(),
            P(),
            P(),
            P(("site", "pt"), "var", None, "cmp"),
        ),
        out_specs=P(("site", "pt"), "var", None, "cmp"),
        check_vma=False,
    )
```

```python
import functools
import math

import jax
import jax.numpy as jnp
import numpy as np
from jax import lax
from jax.experimental import pallas as pl
from jax.experimental.pallas import tpu as pltpu
from jax.sharding import PartitionSpec as P

taper_width = 8.0
MESH = pl.DeviceIdType.MESH
VMEM = pltpu.VMEM
SMEM = pltpu.SMEM


def column_bins(bins_here):
    half = bins_here // 2
    column = np.arange(2 * bins_here)
    return (column // bins_here) * half + column % half, (column // half) % 2


def basis_tables(bins_here, parts, samples):
    bins, imaginary = column_bins(bins_here)
    time = np.arange(samples)[:, None]
    tables = []
    for part in range(parts):
        angle = ((part * bins_here + bins)[None, :] * time % samples) * (2.0 * math.pi / samples)
        tables.append(np.where(imaginary[None, :] == 1, -np.sin(angle), np.cos(angle)))
    exact = np.stack(tables)
    upper = exact.astype(jnp.bfloat16)
    lower = (exact - upper.astype(np.float64)).astype(jnp.bfloat16)
    return np.stack([upper, lower], axis=1)


def wide_dot(rows, upper, lower, dims):
    head = rows.astype(jnp.bfloat16)
    tail = (rows - head.astype(jnp.float32)).astype(jnp.bfloat16)
    dot = functools.partial(
        lax.dot_general, dimension_numbers=(dims, ((), ())), preferred_element_type=jnp.float32
    )
    return dot(head, upper) + (dot(head, lower) + dot(tail, upper))


def hail(peers):
    barrier = pltpu.get_barrier_semaphore()
    for peer in peers:
        pl.semaphore_signal(barrier, inc=1, device_id=peer, device_id_type=MESH)


def await_all(peers):
    pl.semaphore_wait(pltpu.get_barrier_semaphore(), len(peers))


def greet(peers):
    hail(peers)
    await_all(peers)


def others(me, count):
    return [{"pt": lax.rem(me + step, count)} for step in range(1, count)]


def gather_kernel(
    count,
    row_ref,
    blocks_ref,
    covered_ref,
    crossover_ref,
    strain_ref,
    scale_hbm,
    mechanism_hbm,
    slip_hbm,
    onset_hbm,
    band_hbm,
    table_hbm,
    weights_ref,
    slips_ref,
    onsets_ref,
    spectrum_ref,
    band_send,
    final_table,
    weight_ref,
    scale_ref,
    mechanism_ref,
    slip_ref,
    onset_ref,
    band_ref,
    strain_buf,
    wide_buf,
    table_buf,
    band_peer,
    slip_pack,
    onset_pack,
    local_sem,
    load_sem,
    strain_sem,
    send_sem,
    recv_sem,
    pass_sem,
    passed_sem,
):
    me = lax.axis_index("pt")
    part = lax.axis_index("cmp")
    partner = {"cmp": 1 - part}
    blocks_here = scale_ref.shape[0]
    block = strain_ref.shape[0] // blocks_here
    bins = strain_ref.shape[2]
    half = bins // 2
    own = band_ref.shape[3]
    variations = band_ref.shape[1]
    samples = own * final_table.shape[0]
    peers = others(me, count)
    hail(peers + [partner])
    loads = []
    for k, (source, target) in enumerate(
        (
            (slip_hbm, slip_ref),
            (onset_hbm, onset_ref),
            (band_hbm, band_ref),
            (mechanism_hbm, mechanism_ref),
            (scale_hbm, scale_ref),
        )
    ):
        copy = pltpu.make_async_copy(source, target, load_sem.at[k])
        copy.start()
        loads.append(copy)
    strain_copies = []
    for b in range(blocks_here):
        rows = pl.ds(b * block, block)
        copy = pltpu.make_async_copy(strain_ref.at[rows], strain_buf.at[rows], strain_sem.at[b])
        copy.start()
        strain_copies.append(copy)
    table_copy = pltpu.make_async_copy(table_hbm.at[part], table_buf, local_sem.at[0])
    table_copy.start()
    mine = pl.ds(pl.multiple_of(part * own, own), own)
    theirs = pl.ds(pl.multiple_of((1 - part) * own, own), own)
    final_copies = []
    for p in range(final_table.shape[0]):
        for which in range(2):
            copy = pltpu.make_async_copy(
                table_hbm.at[p, which, mine], final_table.at[p, which], local_sem.at[1 + 2 * p + which]
            )
            copy.start()
            final_copies.append(copy)
    loads[0].wait()
    loads[1].wait()
    rupture = row_ref[me]
    covered = covered_ref[rupture]
    spread = variations // 2
    first_part = part == 0

    slot_total = blocks_ref.shape[1]
    whole = [
        (
            onset_ref[0, :, slot * block : (slot + 1) * block],
            slip_ref[0, :, slot * block : (slot + 1) * block].astype(jnp.float32),
        )
        for slot in range(slot_total)
    ]
    halved = [
        tuple(jnp.where(first_part, tile[:spread], tile[spread:]) for tile in pair)
        for pair in whole
    ]

    def packed(target, tiles):
        lowest = target * blocks_here
        totals = [[jnp.zeros_like(tile) for tile in tiles[0]] for k in range(blocks_here)]
        found = jnp.int32(0)
        for slot in range(slot_total):
            named = blocks_ref[rupture, slot]
            live = (slot < covered) & (named >= lowest) & (named < lowest + blocks_here)
            for k in range(min(blocks_here, slot + 1)):
                share = (live & (found == k)).astype(jnp.int32).astype(jnp.float32)
                for which in range(2):
                    totals[k][which] = totals[k][which] + share * tiles[slot][which]
            found = found + live.astype(jnp.int32)
        return totals

    def pack(step, carry):
        for k, (onset, slip) in enumerate(packed(lax.rem(me + 1 + step, count), halved)):
            onset_pack[step, k] = onset
            slip_pack[step, k] = slip.astype(slip_pack.dtype)
        return carry

    lax.fori_loop(0, count - 1, pack, 0)
    await_all(peers + [partner])
    sends = []
    for step, peer in enumerate(peers):
        for which, (source, target) in enumerate(((onset_pack, onsets_ref), (slip_pack, slips_ref))):
            copy = pltpu.make_async_remote_copy(
                src_ref=source.at[step],
                dst_ref=target.at[me, part],
                send_sem=send_sem.at[2 * step + which],
                recv_sem=recv_sem.at[2 * step + which],
                device_id=peer,
                device_id_type=MESH,
            )
            copy.start()
            sends.append(copy)
    loads[2].wait()
    for c in range(2):
        band_send[pl.ds(c * variations, variations), :] = band_ref[0, :, c, :]
    band_copy = pltpu.make_async_remote_copy(
        src_ref=band_send,
        dst_ref=band_peer,
        send_sem=send_sem.at[2 * (count - 1)],
        recv_sem=recv_sem.at[2 * (count - 1)],
        device_id=partner,
        device_id_type=MESH,
    )
    band_copy.start()
    for k, (onset, slip) in enumerate(packed(me, whole)):
        for h in range(2):
            slips_ref[me, h, k] = slip[h * spread : (h + 1) * spread].astype(slips_ref.dtype)
            onsets_ref[me, h, k] = onset[h * spread : (h + 1) * spread]

    crossing = crossover_ref[rupture].astype(jnp.float32)
    column = lax.broadcasted_iota(jnp.int32, weight_ref.shape, 1)
    frequency_id = part * bins + (column // bins) * half + column % half
    frequency = frequency_id.astype(jnp.float32)
    taper = jnp.clip((crossing - frequency) / taper_width + 0.5, 0.0, 1.0)
    weight_ref[...] = taper * jnp.where(frequency_id == 0, 1.0, 2.0) / samples
    loads[3].wait()
    loads[4].wait()
    low_lanes = lax.broadcasted_iota(jnp.int32, (block, bins), 1) < half
    for b in range(blocks_here):
        strain_copies[b].wait()
        wide_buf[...] = (
            strain_buf[pl.ds(b * block, block)].astype(jnp.float32).reshape(block * 24, bins)
        )
        moment = mechanism_ref[:, pl.ds(b * block, block)]
        factors = jnp.transpose(jnp.concatenate([moment] * 4, axis=0)) * scale_ref[pl.ds(b, 1), :]
        for c in range(2):
            green = []
            for ri in range(2):
                total = None
                for j in range(6):
                    row = 12 * ri + 6 * c + j
                    term = factors[:, row : row + 1] * wide_buf[pl.ds(row, block, stride=24), :]
                    total = term if total is None else total + term
                green.append(total)
            real, imag = green
            real_turned = pltpu.roll(real, half, 1)
            imag_turned = pltpu.roll(imag, half, 1)
            lanes = pl.ds(c * bins, bins)
            pieces = (
                (0, 0, real, imag_turned),
                (0, 1, imag, -real_turned),
                (1, 0, real_turned, imag),
                (1, 1, imag_turned, -real),
            )
            for which, lower, first, second in pieces:
                weights_ref[b, which, pl.ds(lower * block, block), lanes] = jnp.where(
                    low_lanes, first, second
                ).astype(jnp.bfloat16)

    passes = []
    for step in range(count - 1):
        source_row = lax.rem(me + count - 1 - step, count)
        for which, target in enumerate((onsets_ref, slips_ref)):
            sends[2 * step + which].wait_recv()
            held = target.at[source_row, part]
            copy = pltpu.make_async_remote_copy(
                src_ref=held,
                dst_ref=held,
                send_sem=pass_sem.at[2 * step + which],
                recv_sem=passed_sem.at[2 * step + which],
                device_id=partner,
                device_id_type=MESH,
            )
            copy.start()
            passes.append(copy)
    table_copy.wait()
    band_copy.wait()
    down = ((1,), (0,))
    spectrum_ref[...] = wide_dot(
        band_send[...], table_buf[0, mine, :], table_buf[1, mine, :], down
    ) + wide_dot(band_peer[...], table_buf[0, theirs, :], table_buf[1, theirs, :], down)
    for copy in final_copies:
        copy.wait()
    for copy in sends:
        copy.wait_send()
    for copy in passes:
        copy.wait()


def turn(first, second):
    return (
        first[0] * second[0] - first[1] * second[1],
        first[0] * second[1] + first[1] * second[0],
    )


def pair_kernel(
    step_angle,
    row_ref,
    blocks_ref,
    covered_ref,
    weights_ref,
    slips_ref,
    onsets_ref,
    partial_ref,
    total_ref,
):
    me = lax.axis_index("pt")
    part = lax.axis_index("cmp")
    blocks_here, halves, depth, columns = weights_ref.shape
    rows, shares, unused, spread, block = slips_ref.shape
    variations = shares * spread
    bins = columns // 2
    half = bins // 2
    fine_total = 16
    lowest = me * blocks_here
    lane_bin = lax.broadcasted_iota(jnp.int32, (variations, columns), 1) % half

    def one_row(row, carry):
        rupture = row_ref[row]
        total_ref[...] = jnp.zeros_like(total_ref)

        def one_slot(slot, found_here):
            local = blocks_ref[rupture, slot] - lowest
            live = (local >= 0) & (local < blocks_here)

            @pl.when(live)
            def _():
                angle = step_angle * jnp.concatenate(
                    [onsets_ref[row, h, found_here] for h in range(shares)], axis=0
                )
                amplitude = jnp.concatenate(
                    [slips_ref[row, h, found_here].astype(jnp.float32) for h in range(shares)],
                    axis=0,
                )
                powers = [None, (jnp.cos(angle), jnp.sin(angle))]
                for k in range(2, fine_total + 1):
                    powers.append(turn(powers[k // 2], powers[k - k // 2]))
                leap = powers[fine_total]
                far = leap
                for unused in range(int(math.log2(bins // fine_total))):
                    far = turn(far, far)
                second_part = part == 1
                coarse = (
                    amplitude * jnp.where(second_part, far[0], 1.0),
                    amplitude * jnp.where(second_part, far[1], 0.0),
                )
                per_half = half // fine_total
                for which in range(halves):
                    found = jnp.zeros((variations, columns), jnp.float32)
                    for h in range(per_half):
                        pieces = []
                        for k in range(fine_total):
                            phase = coarse if k == 0 else turn(coarse, powers[k])
                            pieces.append(
                                jnp.concatenate(
                                    [phase[0].astype(jnp.bfloat16), phase[1].astype(jnp.bfloat16)],
                                    axis=1,
                                )
                            )
                        product = jnp.dot(
                            jnp.concatenate(pieces, axis=0),
                            weights_ref[local, which],
                            preferred_element_type=jnp.float32,
                        )
                        for k in range(fine_total):
                            found = jnp.where(
                                lane_bin == h * fine_total + k,
                                product[k * variations : (k + 1) * variations],
                                found,
                            )
                        coarse = turn(coarse, leap)
                    total_ref[which] += found

            return found_here + live.astype(jnp.int32)

        lax.fori_loop(0, covered_ref[rupture], one_slot, jnp.int32(0))
        partial_ref[row] = total_ref[...].astype(jnp.bfloat16)
        return carry

    lax.fori_loop(0, rows, one_row, 0)


def merge_kernel(
    count,
    partial_ref,
    weight_ref,
    spectrum_ref,
    excess_ref,
    arrived,
    excess_send,
    send_sem,
    recv_sem,
):
    me = lax.axis_index("pt")
    part = lax.axis_index("cmp")
    partner = {"cmp": 1 - part}
    bins = partial_ref.shape[3] // 2
    variations = partial_ref.shape[2]
    greet(others(me, count) + [partner])
    sends = []
    for step, peer in enumerate(others(me, count)):
        copy = pltpu.make_async_remote_copy(
            src_ref=partial_ref.at[peer["pt"]],
            dst_ref=arrived.at[step],
            send_sem=send_sem.at[step],
            recv_sem=recv_sem.at[step],
            device_id=peer,
            device_id_type=MESH,
        )
        copy.start()
        sends.append(copy)
    weight = weight_ref[...]
    total = partial_ref[me].astype(jnp.float32)
    for step, copy in enumerate(sends):
        copy.wait_recv()
        total = total + arrived[step].astype(jnp.float32)
    for c in range(2):
        lanes = slice(c * bins, (c + 1) * bins)
        here = pl.ds(c * variations, variations)
        spectrum = jnp.concatenate([total[0][:, lanes], total[1][:, lanes]], axis=1)
        excess_send[here, :] = (spectrum - spectrum_ref[here, :]) * weight
    exchange = pltpu.make_async_remote_copy(
        src_ref=excess_send,
        dst_ref=excess_ref.at[1],
        send_sem=send_sem.at[count - 1],
        recv_sem=recv_sem.at[count - 1],
        device_id=partner,
        device_id_type=MESH,
    )
    exchange.start()
    excess_ref[0] = excess_send[...]
    for copy in sends:
        copy.wait_send()
    exchange.wait()


def final_kernel(excess_ref, band_ref, table_ref, out_ref):
    part = lax.axis_index("cmp")
    variations = out_ref.shape[1]
    across = ((1,), (1,))
    low = band_ref[...]
    for which in range(2):
        source = lax.rem(part + which, 2)
        low = low + wide_dot(
            excess_ref[which], table_ref[source, 0], table_ref[source, 1], across
        )
    for c in range(2):
        out_ref[0, :, c, :] = low[c * variations : (c + 1) * variations]


def stay(array):
    return pltpu.with_memory_space_constraint(array, VMEM)


def body(
    strain_green,
    green_scale,
    mechanism,
    slip_amplitude,
    onset_time,
    rupture_row,
    rupture_blocks,
    block_count,
    crossover,
    high_band,
):
    points, unused, bins = strain_green.shape
    blocks_here = green_scale.shape[0]
    block = points // blocks_here
    rows_here, variations, slots = slip_amplitude.shape
    count = lax.axis_size("pt")
    parts = lax.axis_size("cmp")
    own = high_band.shape[3]
    samples = own * parts
    rows = rows_here * count
    tables = jnp.asarray(basis_tables(bins, parts, samples))
    vmem = pl.BlockSpec(memory_space=VMEM)
    smem = pl.BlockSpec(memory_space=SMEM)
    anywhere = pl.BlockSpec(memory_space=pltpu.HBM)
    grant = 24 * 1024 * 1024
    copies = 2 * (count - 1) + 1
    share = (blocks_here, variations // 2, block)
    weights, slips, onsets, band_spectrum, band_rows, final_table, weight = pl.pallas_call(
        functools.partial(gather_kernel, count),
        out_shape=(
            VMEM((blocks_here, 2, 2 * block, 2 * bins), jnp.bfloat16),
            VMEM((rows, 2) + share, slip_amplitude.dtype),
            VMEM((rows, 2) + share, onset_time.dtype),
            VMEM((2 * variations, 2 * bins), jnp.float32),
            VMEM((2 * variations, own), jnp.float32),
            VMEM((parts, 2, own, 2 * bins), jnp.bfloat16),
            VMEM((variations, 2 * bins), jnp.float32),
        ),
        in_specs=[smem] * 4 + [anywhere] * 7,
        out_specs=(vmem,) * 7,
        scratch_shapes=[
            VMEM(green_scale.shape, green_scale.dtype),
            VMEM(mechanism.shape, mechanism.dtype),
            VMEM(slip_amplitude.shape, slip_amplitude.dtype),
            VMEM(onset_time.shape, onset_time.dtype),
            VMEM(high_band.shape, high_band.dtype),
            VMEM(strain_green.shape, strain_green.dtype),
            VMEM((block * 24, bins), jnp.float32),
            VMEM((2, samples, 2 * bins), jnp.bfloat16),
            VMEM((2 * variations, own), jnp.float32),
            VMEM((count - 1,) + share, slip_amplitude.dtype),
            VMEM((count - 1,) + share, onset_time.dtype),
            pltpu.SemaphoreType.DMA((1 + 2 * parts,)),
            pltpu.SemaphoreType.DMA((5,)),
            pltpu.SemaphoreType.DMA((blocks_here,)),
            pltpu.SemaphoreType.DMA((copies,)),
            pltpu.SemaphoreType.DMA((copies,)),
            pltpu.SemaphoreType.DMA((copies - 1,)),
            pltpu.SemaphoreType.DMA((copies - 1,)),
        ],
        compiler_params=pltpu.CompilerParams(collective_id=0, has_side_effects=True),
        name="gather",
    )(
        rupture_row,
        rupture_blocks,
        block_count,
        crossover,
        strain_green,
        green_scale,
        mechanism,
        slip_amplitude,
        onset_time,
        high_band,
        tables,
    )
    partial_spectra = pl.pallas_call(
        functools.partial(pair_kernel, 2.0 * math.pi / samples),
        out_shape=VMEM((rows, 2, variations, 2 * bins), jnp.bfloat16),
        in_specs=[smem, smem, smem, vmem, vmem, vmem],
        out_specs=vmem,
        scratch_shapes=[VMEM((2, variations, 2 * bins), jnp.float32)],
        compiler_params=pltpu.CompilerParams(vmem_limit_bytes=grant),
        name="pairs",
    )(rupture_row, rupture_blocks, block_count, stay(weights), stay(slips), stay(onsets))
    excess = pl.pallas_call(
        functools.partial(merge_kernel, count),
        out_shape=VMEM((2, 2 * variations, 2 * bins), jnp.float32),
        in_specs=[vmem, vmem, vmem],
        out_specs=vmem,
        scratch_shapes=[
            VMEM((count - 1, 2, variations, 2 * bins), jnp.bfloat16),
            VMEM((2 * variations, 2 * bins), jnp.float32),
            pltpu.SemaphoreType.DMA((count,)),
            pltpu.SemaphoreType.DMA((count,)),
        ],
        compiler_params=pltpu.CompilerParams(collective_id=1, has_side_effects=True, vmem_limit_bytes=grant),
        name="merge",
    )(stay(partial_spectra), stay(weight), stay(band_spectrum))
    return pl.pallas_call(
        final_kernel,
        out_shape=jax.ShapeDtypeStruct(high_band.shape, high_band.dtype),
        in_specs=[vmem, vmem, vmem],
        out_specs=vmem,
        compiler_params=pltpu.CompilerParams(vmem_limit_bytes=grant),
        name="final",
    )(stay(excess), stay(band_rows), stay(final_table))


def solution(mesh):
    return jax.shard_map(
        body,
        mesh=mesh,
        in_specs=(
            P(("site", "pt"), None, "cmp"),
            P(("site", "pt"), None),
            P(None, "pt"),
            P("pt", "var", None),
            P("pt", "var", None),
            P(),
            P(),
            P(),
            P(),
            P(("site", "pt"), "var", None, "cmp"),
        ),
        out_specs=P(("site", "pt"), "var", None, "cmp"),
        check_vma=False,
    )
```
